128 devices in a mesh: group: 4 (over y), ctx: 32 (over x, z, core).
Axes of the slice: x: 4, y: 4, z: 4, core: 2. Of those that a mesh axis runs over, the one named last changes fastest.
Arguments:
- query: bfloat16 [128, 128, 576], P('group', 'ctx'), may hold values from -160 to 160
- cache: bfloat16 [32, 32768, 576], P('group', 'ctx'), may hold values from -6 to 6
- new_keys: bfloat16 [128, 576], P('group'), may hold values from -7 to 7
- lengths: int32 [32], P('group'), may hold values from 1 to 32768, as said below
- value_up_weight: bfloat16 [128, 512, 128], P('ctx'), may hold values from -1 to 1
- w_out: bfloat16 [16384, 7168], P('ctx'), may hold values from -0.1875 to 0.1875
- residual: bfloat16 [128, 7168], P(('group', 'ctx')), may hold values from -6 to 6
- norm_gain: float32 [7168], replicated, may hold values from 0.1 to 1.9
- w_router: bfloat16 [7168, 16], replicated, may hold values from -0.125 to 0.125
- routes: int32 [128, 8], P(('group', 'ctx')), may hold values from 0 to 15, all different within a row
- w_gate: bfloat16 [7168, 32768], P(None, ('group', 'ctx')), may hold values from -0.0625 to 0.0625
- w_up: bfloat16 [7168, 32768], P(None, ('group', 'ctx')), may hold values from -0.0625 to 0.0625
- w_down: bfloat16 [32768, 7168], P(('group', 'ctx')), may hold values from -0.125 to 0.125
Outputs:
- attn_out: bfloat16 [128, 7168], P(('group', 'ctx'))
- layer_out: bfloat16 [128, 7168], P(('group', 'ctx'))
The draws below stay inside these ranges and needn't reach their ends.
Inputs may be any that keep to these rules, and one draw needn't show every extreme that they name: `lengths`: some request has all 32768 positions live.
All inputs are finite; a program needn't handle non-finite values.
Results may differ from the reference program's by a relative error of at most 0.018.
Values may be sent and summed in bfloat16 or wider, within the bound.
No kernel may reach another device: no remote copies, remote signals or barrier semaphores. Data moves between devices by JAX's collectives and lax.ppermute only.
A program may use at most 192 MiB of HBM per device.

```python
import jax
import jax.numpy as jnp
from jax import lax

D = 7168
HEAD_COUNT = 128
LATENT_WIDTH = 512
ROTARY_WIDTH = 64
QK_NOPE = 128
VALUE_HEAD_WIDTH = 128
FF_E = 2048
TOPK = 8
EXPERTS = 16
QPR = 4
S_DEV = 1024
LAT = 576
REQS = 32
QUERY_ROW_TOTAL = 128
LEN = 32768
N_CTX = 32


def draw_query(key, part):
    noise_key = jax.random.fold_in(key, 1)
    value_rows = jnp.clip(jax.random.normal(noise_key, (QUERY_ROW_TOTAL, HEAD_COUNT, LAT), jnp.float32), -5.0, 5.0) * 0.8
    return value_rows.astype(jnp.bfloat16)


def draw_cache(key, part):
    noise_key = jax.random.fold_in(key, 2)
    value_rows = jnp.clip(jax.random.normal(noise_key, (REQS, LEN, LAT), jnp.float32), -5.0, 5.0)
    return value_rows.astype(jnp.bfloat16)


def draw_new_keys(key, part):
    noise_key = jax.random.fold_in(key, 3)
    value_rows = jnp.clip(jax.random.normal(noise_key, (QUERY_ROW_TOTAL, LAT), jnp.float32), -5.0, 5.0)
    return value_rows.astype(jnp.bfloat16)


def draw_lengths(key, part):
    length_key, second = jax.random.split(jax.random.fold_in(key, 4))
    value_rows = jax.random.randint(length_key, (REQS,), 1, LEN + 1, dtype=jnp.int32)
    long_spot = jax.random.randint(second, (), 0, REQS, dtype=jnp.int32)
    return jnp.where(jnp.arange(REQS, dtype=jnp.int32) == long_spot, LEN, value_rows).astype(jnp.int32)


def steps_of(key, dims, shards, least, top_value):
    def one(position, parts):
        draws = jax.random.uniform(jax.random.fold_in(jax.random.fold_in(key, 6), position), (parts,), jnp.float32, least / len(shards), top_value / len(shards))
        return jnp.repeat(jnp.exp(draws), dims[position] // parts).reshape((-1,) + (1,) * (len(dims) - position - 1))

    gain = one(*shards[0])
    for cut in shards[1:]:
        gain = gain * one(*cut)
    return gain


def picks_of(rng, rows, number_of, top, lift):
    sequence = jax.random.permutation(jax.random.fold_in(rng, 1), number_of)
    favour = sequence
    for power in range(3):
        favour = favour * favour // number_of
    favour = favour * lift // number_of
    tickets = jax.random.randint(jax.random.fold_in(rng, 2), (rows, number_of), 0, 4096) + favour
    fixed_rows = jax.random.permutation(jax.random.fold_in(rng, 3), rows)[jnp.arange(number_of) % rows]
    tickets = jnp.where(jnp.arange(rows)[:, None] == fixed_rows[None, :], 1 << 14, tickets)
    merit = tickets * number_of + jnp.arange(number_of)
    return lax.top_k(merit.astype(jnp.int32), top)[1].astype(jnp.int32)


def scatter_about(rng, shape, spread, reach, cuts=(), held_as=jnp.bfloat16):
    array = jax.random.normal(rng, shape, jnp.float32) * spread
    if len(cuts) > 0:
        array = steps_of(rng, shape, cuts, -0.22, 0.18) * array
    return jnp.clip(array, min=-reach, max=reach).astype(held_as)


def setup_inputs(seed: int = 0) -> dict:
    key_of = jax.random.split(jax.random.key(seed), 14)
    query = draw_query(jax.random.fold_in(key_of[13], 71), 0)
    cache = draw_cache(jax.random.fold_in(key_of[13], 71), 0)
    new_keys = draw_new_keys(jax.random.fold_in(key_of[13], 71), 0)
    lengths = draw_lengths(jax.random.fold_in(key_of[13], 71), 0)
    value_up_weight = scatter_about(key_of[4], (HEAD_COUNT, LATENT_WIDTH, VALUE_HEAD_WIDTH), (LATENT_WIDTH // 16) ** -0.5, 1.0, ((0, 32),))
    w_out = scatter_about(key_of[5], (HEAD_COUNT * VALUE_HEAD_WIDTH, D), (HEAD_COUNT * VALUE_HEAD_WIDTH // 16) ** -0.5, 0.1875, ((0, 32),))
    residual = scatter_about(key_of[6], (QUERY_ROW_TOTAL, D), 1.0, 6.0, ((0, 128),))
    norm_gain = jnp.clip(1.0 + 0.18 * jax.random.normal(key_of[7], (D,), jnp.float32), 0.1, 1.9)
    w_router = scatter_about(key_of[8], (D, EXPERTS), (D // 4) ** -0.5, 0.125)
    routes = picks_of(key_of[9], QUERY_ROW_TOTAL, EXPERTS, TOPK, 4096)
    w_gate = scatter_about(key_of[10], (D, EXPERTS * FF_E), D ** -0.5, 0.0625, ((1, 128),))
    w_up = scatter_about(key_of[11], (D, EXPERTS * FF_E), D ** -0.5, 0.0625, ((1, 128),))
    w_down = scatter_about(key_of[12], (EXPERTS * FF_E, D), FF_E ** -0.5, 0.125, ((0, 128),))
    return {"query": query, "cache": cache, "new_keys": new_keys, "lengths": lengths, "value_up_weight": value_up_weight, "w_out": w_out, "residual": residual, "norm_gain": norm_gain, "w_router": w_router, "routes": routes, "w_gate": w_gate, "w_up": w_up, "w_down": w_down}


neg_floor = -1e+30
route_scale = 2.5
norm_eps = 1e-06

def request_latent(query_rows, cache_rows, recent_keys, length):
    score_scale = (QK_NOPE + ROTARY_WIDTH) ** (-0.5)
    query_wide = query_rows.astype(jnp.float32)
    block_list = cache_rows.reshape(N_CTX, S_DEV, LAT).astype(jnp.float32)
    positions = jnp.arange(LEN, dtype=jnp.int32).reshape(N_CTX, S_DEV)
    live_mask = (positions < length)[:, None, None, :]
    scores = score_scale * jnp.einsum('qhd,btd->bqht', query_wide, block_list, precision=lax.Precision.HIGHEST)
    block_max = lax.optimization_barrier(jnp.max(jnp.where(live_mask, scores, neg_floor), axis=-1))
    probability = jnp.exp(jnp.where(live_mask, scores - block_max[..., None], neg_floor))
    block_sum = lax.optimization_barrier(jnp.sum(probability, axis=-1))
    rounded_width = lax.optimization_barrier(probability.astype(jnp.bfloat16)).astype(jnp.float32)
    block_result = jnp.einsum('arij,ajx->arix', rounded_width, block_list[:, :, :LATENT_WIDTH], precision=lax.Precision.HIGHEST)
    recent_wide_keys = recent_keys.astype(jnp.float32)
    near_scores = score_scale * jnp.einsum('qhd,jd->qhj', query_wide, recent_wide_keys, precision=lax.Precision.HIGHEST)
    causal = (jnp.arange(QPR, dtype=jnp.int32)[None, :] <= jnp.arange(QPR, dtype=jnp.int32)[:, None])[:, None, :]
    near_max = lax.optimization_barrier(jnp.max(jnp.where(causal, near_scores, neg_floor), axis=-1))
    joint_max = jnp.maximum(lax.optimization_barrier(jnp.max(block_max, axis=0)), near_max)
    block_rescale = jnp.exp(block_max - joint_max[None])
    nearby_probability = jnp.exp(jnp.where(causal, near_scores - joint_max[..., None], neg_floor))
    denominator = lax.optimization_barrier(jnp.sum(block_rescale * block_sum, axis=0)) + lax.optimization_barrier(jnp.sum(nearby_probability, axis=-1))
    softmax_numerator = lax.optimization_barrier(jnp.sum(block_rescale[..., None] * block_result, axis=0)) + jnp.einsum('pbl,lv->pbv', nearby_probability, recent_wide_keys[:, :LATENT_WIDTH], precision=lax.Precision.HIGHEST)
    return (softmax_numerator / denominator[..., None]).astype(jnp.bfloat16)

def reference(query, cache, new_keys, lengths, value_up_weight, w_out, residual, norm_gain, w_router, routes, w_gate, w_up, w_down):
    query_grid = query.reshape(REQS, QPR, HEAD_COUNT, LAT)
    fresh_grid = new_keys.reshape(REQS, QPR, LAT)
    latent_vector = lax.map(lambda packed: request_latent(packed[0], packed[1], packed[2], packed[3]), (query_grid, cache, fresh_grid, lengths))
    latent_vector = latent_vector.reshape(QUERY_ROW_TOTAL, HEAD_COUNT, LATENT_WIDTH)
    per_head_values = jnp.einsum('gxj,xjs->gxs', latent_vector.astype(jnp.float32), value_up_weight.astype(jnp.float32), precision=lax.Precision.HIGHEST).astype(jnp.bfloat16)
    attention = jnp.dot(per_head_values.reshape(QUERY_ROW_TOTAL, HEAD_COUNT * VALUE_HEAD_WIDTH), w_out, preferred_element_type=jnp.float32)
    attn_out = attention.astype(jnp.bfloat16)
    stream = (residual.astype(jnp.float32) + attention).astype(jnp.bfloat16)
    stream_wide = stream.astype(jnp.float32)
    mean_square = lax.optimization_barrier(jnp.mean(stream_wide * stream_wide, axis=-1, keepdims=True))
    normed = (stream_wide * lax.rsqrt(mean_square + norm_eps) * norm_gain).astype(jnp.bfloat16)
    gate_values = jax.nn.sigmoid(jnp.dot(normed, w_router, preferred_element_type=jnp.float32))
    selected_experts = (routes[:, :, None] == jnp.arange(EXPERTS, dtype=jnp.int32)[None, None, :]).astype(jnp.float32)
    picked = lax.optimization_barrier(jnp.sum(selected_experts * gate_values[:, None, :], axis=-1))
    route_weights = route_scale * picked / lax.optimization_barrier(jnp.sum(picked, axis=-1, keepdims=True))
    coefficient = lax.optimization_barrier(jnp.sum(route_weights[:, :, None] * selected_experts, axis=1))
    expert_mix = jnp.zeros((QUERY_ROW_TOTAL, D), jnp.float32)
    for expert in range(EXPERTS):
        columns = slice(expert * FF_E, (expert + 1) * FF_E)
        gate_sum = jnp.dot(normed, w_gate[:, columns], preferred_element_type=jnp.float32)
        up_sum = jnp.dot(normed, w_up[:, columns], preferred_element_type=jnp.float32)
        hidden = (jax.nn.silu(gate_sum) * up_sum).astype(jnp.bfloat16)
        expert_out = jnp.dot(hidden, w_down[columns, :], preferred_element_type=jnp.float32)
        expert_mix = expert_mix + coefficient[:, expert:expert + 1] * expert_out
    layer_out = (stream_wide + expert_mix).astype(jnp.bfloat16)
    return (attn_out, layer_out)
```

```python
import functools

import jax
import jax.numpy as jnp
from jax import lax
from jax.experimental import pallas as pl
from jax.experimental.pallas import tpu as pltpu
from jax.sharding import Mesh, PartitionSpec as P

LATENT_WIDTH = 512
ROTARY_WIDTH = 64
QK_NOPE = 128
VALUE_HEAD_WIDTH = 128
EXPERTS = 16
LANES = 128
STAT = 16

neg_floor = -1e30
route_scale = 2.5
norm_eps = 1e-06
score_scale = (QK_NOPE + ROTARY_WIDTH) ** (-0.5)
f32 = jnp.float32
bf16 = jnp.bfloat16


def split3(value):
    high = value.astype(bf16).astype(f32)
    rest = value - high
    middle = rest.astype(bf16).astype(f32)
    return high, middle, (rest - middle).astype(bf16).astype(f32)


def place(stat_lanes, column, request, base):
    lane = lax.broadcasted_iota(jnp.int32, stat_lanes.shape, 1)
    for part, piece in enumerate(split3(column)):
        stat_lanes = jnp.where(lane == base + part * STAT + request, piece, stat_lanes)
    return stat_lanes


def join3(tile):
    return tile + pltpu.roll(tile, LANES - STAT, 1) + pltpu.roll(tile, LANES - 2 * STAT, 1)


def attend_kernel(blocks_ref, lengths_ref, q0, q1, q2, q3, own_ref, sib_ref, o0, o1, o2, o3, stat_ref, *, first, count):
    step = pl.program_id(0)
    length = lengths_ref[first + step]
    outs = (o0, o1, o2, o3)
    query = jnp.concatenate([ref[...].reshape(-1, ref.shape[-1]) for ref in (q0, q1, q2, q3)], axis=0)
    rows = query.shape[0]
    block_len = own_ref.shape[2]
    scores = []
    for which, keys in enumerate((own_ref, sib_ref)):
        score = score_scale * jnp.dot(query, keys[0], preferred_element_type=f32)
        position = blocks_ref[which] * block_len + lax.broadcasted_iota(jnp.int32, (1, block_len), 1)
        scores.append(jnp.where(position < length, score, neg_floor))
    top = jnp.maximum(
        jnp.max(scores[0], axis=-1, keepdims=True), jnp.max(scores[1], axis=-1, keepdims=True)
    )
    shift = jnp.where(top <= neg_floor, 0.0, top)
    total = jnp.zeros((rows, 1), f32)
    result = jnp.zeros((rows, LATENT_WIDTH), f32)
    for score, keys in zip(scores, (own_ref, sib_ref)):
        probability = jnp.exp(score - shift)
        total = total + jnp.sum(probability, axis=-1, keepdims=True)
        result = result + lax.dot_general(
            probability.astype(bf16),
            keys[0, :LATENT_WIDTH],
            (((1,), (1,)), ((), ())),
            preferred_element_type=f32,
        )

    @pl.when(step == 0)
    def _():
        stat_ref[...] = jnp.zeros_like(stat_ref)

    stats = place(place(stat_ref[...], top, step, 0), total, step, 3 * STAT)
    stat_ref[...] = stats
    part = rows // 4
    pieces = part // 16
    for d, out in enumerate(outs):
        for chunk in range(LATENT_WIDTH // LANES):
            tile = result[d * part : (d + 1) * part, chunk * LANES : (chunk + 1) * LANES]
            out[:, step * 4 + chunk] = tile.astype(bf16).reshape(pieces, 16, LANES)

    @pl.when(step == count - 1)
    def _():
        for d, out in enumerate(outs):
            out[:, 4 * count] = stats[d * part : (d + 1) * part].astype(bf16).reshape(pieces, 16, LANES)


def attend(blocks, lengths, queries, cache, sibling, first, count):
    features, block_len = cache.shape[1:]
    tiles = 4 * count + 1
    out = jax.ShapeDtypeStruct((4, tiles, 16, LANES), bf16)
    rows = 4 * queries[0].shape[0] * 16
    return pl.pallas_call(
        functools.partial(attend_kernel, first=first, count=count),
        out_shape=[out] * 4,
        grid_spec=pltpu.PrefetchScalarGridSpec(
            num_scalar_prefetch=2,
            grid=(count,),
            in_specs=[pl.BlockSpec((4, None, 16, features), lambda i, *_: (0, i, 0, 0))] * 4
            + [pl.BlockSpec((1, features, block_len), lambda i, *_: (first + i, 0, 0))] * 2,
            out_specs=[pl.BlockSpec((4, tiles, 16, LANES), lambda i, *_: (0, 0, 0, 0))] * 4,
            scratch_shapes=[pltpu.VMEM((rows, LANES), f32)],
        ),
        compiler_params=pltpu.CompilerParams(
            dimension_semantics=("arbitrary",), vmem_limit_bytes=48 << 20
        ),
        name="attend",
    )(blocks, lengths, *queries, cache, sibling)


def merged_stats(tiles):
    joined = [join3(tile) for tile in tiles]
    sums = [pltpu.roll(one, LANES - 3 * STAT, 1) for one in joined]
    top = functools.reduce(jnp.maximum, joined)
    weights = [jnp.exp(one - top) for one in joined]
    total = sum(weight * one for weight, one in zip(weights, sums))
    return weights, top, total


def merge_kernel(a0, a1, a2, a3, o0, o1, o2, o3, *, count):
    refs = (a0, a1, a2, a3)
    for piece, out in enumerate((o0, o1, o2, o3)):
        weights, top, total = merged_stats([ref[piece, 4 * count].astype(f32) for ref in refs])
        stats = jnp.zeros((16, LANES), f32)
        for request in range(count):
            stats = place(stats, top[:, request : request + 1], request, 0)
            stats = place(stats, total[:, request : request + 1], request, 3 * STAT)
            shares = [weight[:, request : request + 1] for weight in weights]
            for chunk in range(4):
                tile = sum(
                    share * ref[piece, 4 * request + chunk].astype(f32)
                    for share, ref in zip(shares, refs)
                )
                out[4 * request + chunk] = tile.astype(bf16)
        out[4 * count] = stats.astype(bf16)


def merge(pieces, count):
    return pl.pallas_call(
        functools.partial(merge_kernel, count=count),
        out_shape=[jax.ShapeDtypeStruct((4 * count + 1, 16, LANES), bf16)] * 4,
        compiler_params=pltpu.CompilerParams(vmem_limit_bytes=32 << 20),
        name="merge",
    )(*pieces)


def project_kernel(core_ref, *refs, count):
    first, second = refs[0:4], refs[4:8]
    q_ref, keys_ref, up_ref, w_hbm, kept_ref, given_ref, w_ref, rows_ref, sems = refs[8:]
    chunk = kept_ref.shape[2]

    def fetch(k):
        window = pl.ds(k * chunk, chunk)
        return pltpu.make_async_copy(w_hbm.at[:, window], w_ref.at[:, window], sems.at[k])

    for k in range(SPAN):
        fetch(k).start()
    tops, totals, results = [], [], []
    for half in (first, second):
        weights, top, total = merged_stats([ref[4 * count].astype(f32) for ref in half])
        for request in range(count):
            tops.append(top[:, request : request + 1])
            totals.append(total[:, request : request + 1])
            shares = [weight[:, request : request + 1] for weight in weights]
            results.append(
                jnp.concatenate(
                    [
                        sum(
                            share * ref[4 * request + part].astype(f32)
                            for share, ref in zip(shares, half)
                        )
                        for part in range(4)
                    ],
                    axis=1,
                )
            )
    cache_max = jnp.concatenate(tops, axis=0)
    cache_sum = jnp.concatenate(totals, axis=0)
    cache_result = jnp.concatenate(results, axis=0)
    rows = cache_max.shape[0]
    keys = keys_ref[...]
    near = score_scale * lax.dot_general(
        q_ref[...].reshape(rows, keys.shape[1]), keys, (((1,), (1,)), ((), ())), preferred_element_type=f32
    )
    row = lax.broadcasted_iota(jnp.int32, near.shape, 0)
    column = lax.broadcasted_iota(jnp.int32, near.shape, 1)
    seen = (row // 16 == column // 4) & (column % 4 <= (row % 16) // 4)
    near = jnp.where(seen, near, neg_floor)
    joint = jnp.maximum(cache_max, jnp.max(near, axis=-1, keepdims=True))
    rescale = jnp.exp(cache_max - joint)
    probability = jnp.where(seen, jnp.exp(near - joint), 0.0)
    denominator = cache_sum * rescale + jnp.sum(probability, axis=-1, keepdims=True)
    near_result = sum(
        jnp.dot(part.astype(bf16), keys[:, :LATENT_WIDTH], preferred_element_type=f32)
        for part in split3(probability)
    )
    latent = ((cache_result * rescale + near_result) / denominator).astype(bf16)
    grouped = rows // 4
    pick_row = lax.broadcasted_iota(jnp.int32, (grouped, rows), 0)
    pick_column = lax.broadcasted_iota(jnp.int32, (grouped, rows), 1)
    halves = grouped // 2
    core = core_ref[0]
    order = 2 * (pick_row % halves) + jnp.where(pick_row < halves, core, 1 - core)
    values = []
    for head in range(4):
        head_value = jnp.dot(latent, up_ref[head], preferred_element_type=f32).astype(bf16)
        pick = (pick_column == 4 * order + head).astype(f32).astype(bf16)
        values.append(jnp.dot(pick, head_value, preferred_element_type=f32).astype(bf16))
    values = jnp.concatenate(values, axis=1)
    for k in range(SPAN):
        fetch(k).wait()
        block = jnp.dot(values, w_ref[:, k * chunk : (k + 1) * chunk], preferred_element_type=f32)
        for piece in range(chunk // LANES):
            rows_ref[piece, pl.ds(k, grouped, stride=SPAN), :] = block[:, piece * LANES : (piece + 1) * LANES]
    for piece in range(chunk // LANES):
        window = slice(piece * LANES, (piece + 1) * LANES)
        whole = rows_ref[piece].reshape(grouped, SPAN, LANES).astype(bf16)
        kept_ref[:, :, window] = whole[:halves]
        given_ref[:, :, window] = whole[halves:]


SPAN = 8


def project(core, first, second, own_query, new_keys, value_up, w_out, count):
    grouped = new_keys.shape[0]
    width = w_out.shape[1]
    out = jax.ShapeDtypeStruct((grouped // 2, SPAN, width // SPAN), bf16)
    inside = pl.BlockSpec(memory_space=pltpu.VMEM)
    return pl.pallas_call(
        functools.partial(project_kernel, count=count),
        out_shape=[out, out],
        in_specs=[pl.BlockSpec(memory_space=pltpu.SMEM)] + [inside] * 11 + [pl.BlockSpec(memory_space=pltpu.HBM)],
        out_specs=[inside] * 2,
        scratch_shapes=[
            pltpu.VMEM(w_out.shape, bf16),
            pltpu.VMEM((width // SPAN // LANES, grouped * SPAN, LANES), f32),
            pltpu.SemaphoreType.DMA((SPAN,)),
        ],
        compiler_params=pltpu.CompilerParams(vmem_limit_bytes=32 << 20),
        name="project",
    )(core, *first, *second, own_query, new_keys, value_up, pltpu.with_memory_space_constraint(w_out, pltpu.HBM))


def spread_kernel(arrived_ref, residual_ref, gain_ref, chosen_ref, attn_ref, stream_ref, rows_ref):
    attention = jnp.sum(arrived_ref[...].astype(f32), axis=0)
    attn_ref[...] = attention.astype(bf16)
    stream = (residual_ref[...].astype(f32) + attention).astype(bf16)
    stream_ref[...] = stream
    wide = stream.astype(f32)
    square = jnp.sum(jnp.sum(wide * wide, axis=1, keepdims=True), axis=0, keepdims=True)
    mean_square = square / (wide.shape[0] * wide.shape[1])
    normed = (wide * lax.rsqrt(mean_square + norm_eps) * gain_ref[...]).astype(bf16)
    row = jnp.concatenate([normed, chosen_ref[...]], axis=1)
    rows_ref[...] = jnp.broadcast_to(row[None], rows_ref.shape)


def spread(arrived, residual, gain, chosen, chips):
    one = jax.ShapeDtypeStruct(residual.shape, bf16)
    rows = jax.ShapeDtypeStruct((chips, SPAN, residual.shape[1] + LANES), bf16)
    return pl.pallas_call(
        spread_kernel,
        out_shape=[one, one, rows],
        compiler_params=pltpu.CompilerParams(vmem_limit_bytes=32 << 20),
        name="spread",
    )(arrived, residual, gain, chosen)


def experts_kernel(
    expert_ref, own_ref, sib_ref, router_ref, gate_hbm, up_hbm, down_hbm, out_own, out_sib,
    gate_ref, up_ref, down_ref, rows_ref, sems
):
    half = own_ref.shape[0]
    rows = 2 * half
    chunk = out_own.shape[2]
    tiles = chunk // LANES

    def fetch(which, k):
        window = pl.ds(k * chunk, chunk)
        source, target = ((gate_hbm, gate_ref), (up_hbm, up_ref), (down_hbm, down_ref))[which]
        if which == 2:
            return pltpu.make_async_copy(source.at[:, window], target.at[:, window], sems.at[which, k])
        return pltpu.make_async_copy(source.at[window], target.at[window], sems.at[which, k])

    for k in range(SPAN):
        fetch(0, k).start()
        fetch(1, k).start()
    for k in range(SPAN):
        fetch(2, k).start()
    for piece in range(tiles):
        window = slice(piece * LANES, (piece + 1) * LANES)
        rows_ref[piece, : half * SPAN] = own_ref[:, :, window].astype(f32).reshape(half * SPAN, LANES)
        rows_ref[piece, half * SPAN :] = sib_ref[:, :, window].astype(f32).reshape(half * SPAN, LANES)
    gate = up = values = 0.0
    for k in range(SPAN):
        block = jnp.concatenate(
            [rows_ref[piece, pl.ds(k, rows, stride=SPAN), :] for piece in range(tiles)], axis=1
        ).astype(bf16)
        values = values + lax.dot_general(
            block,
            router_ref[:, k * chunk : (k + 1) * chunk],
            (((1,), (1,)), ((), ())),
            preferred_element_type=f32,
        )
        fetch(0, k).wait()
        gate = gate + jnp.dot(block, gate_ref[k * chunk : (k + 1) * chunk], preferred_element_type=f32)
        fetch(1, k).wait()
        up = up + jnp.dot(block, up_ref[k * chunk : (k + 1) * chunk], preferred_element_type=f32)
    hidden = (gate / (1.0 + jnp.exp(-gate)) * up).astype(bf16)
    values = 1.0 / (1.0 + jnp.exp(-values))
    chosen = jnp.concatenate(
        [ref[:, :, chunk:].astype(f32).reshape(half * SPAN, LANES) for ref in (own_ref, sib_ref)], axis=0
    )
    rows_ref[0] = chosen
    chosen = rows_ref[0, pl.ds(0, rows, stride=SPAN), :][:, :EXPERTS]
    picked = values * chosen
    lane = lax.broadcasted_iota(jnp.int32, picked.shape, 1)
    mine = jnp.sum(jnp.where(lane == expert_ref[0], picked, 0.0), axis=-1, keepdims=True)
    share = route_scale * mine / jnp.sum(picked, axis=-1, keepdims=True)
    for k in range(SPAN):
        fetch(2, k).wait()
        result = share * jnp.dot(
            hidden, down_ref[:, k * chunk : (k + 1) * chunk], preferred_element_type=f32
        )
        for piece in range(tiles):
            rows_ref[piece, pl.ds(k, rows, stride=SPAN), :] = result[:, piece * LANES : (piece + 1) * LANES]
    for piece in range(tiles):
        window = slice(piece * LANES, (piece + 1) * LANES)
        out_own[:, :, window] = rows_ref[piece, : half * SPAN].reshape(half, SPAN, LANES).astype(bf16)
        out_sib[:, :, window] = rows_ref[piece, half * SPAN :].reshape(half, SPAN, LANES).astype(bf16)


def experts(expert, own_rows, sibling_rows, w_gate, w_up, w_router, w_down):
    width = w_gate.shape[0]
    half = own_rows.shape[0]
    out = jax.ShapeDtypeStruct((half, SPAN, width // SPAN), bf16)
    inside = pl.BlockSpec(memory_space=pltpu.VMEM)
    outside = pl.BlockSpec(memory_space=pltpu.HBM)
    return pl.pallas_call(
        experts_kernel,
        out_shape=[out, out],
        in_specs=[pl.BlockSpec(memory_space=pltpu.SMEM)] + [inside] * 3 + [outside] * 3,
        out_specs=[inside] * 2,
        scratch_shapes=[
            pltpu.VMEM(w_gate.shape, bf16),
            pltpu.VMEM(w_up.shape, bf16),
            pltpu.VMEM(w_down.shape, bf16),
            pltpu.VMEM((width // SPAN // LANES, 2 * half * SPAN, LANES), f32),
            pltpu.SemaphoreType.DMA((3, SPAN)),
        ],
        compiler_params=pltpu.CompilerParams(vmem_limit_bytes=48 << 20),
        name="experts",
    )(expert, own_rows, sibling_rows, w_router.T, w_gate, w_up, w_down)


def shift_by(value, axis, offset):
    size = lax.axis_size(axis)
    return lax.ppermute(value, axis, [(i, (i + offset) % size) for i in range(size)])


def all_shifts(value, axis):
    return [value] + [shift_by(value, axis, d) for d in range(1, lax.axis_size(axis))]


def return_shifts(pieces, axis):
    return [pieces[0]] + [shift_by(piece, axis, -d) for d, piece in enumerate(pieces) if d > 0]


def local(
    query,
    cache,
    new_keys,
    lengths,
    value_up_weight,
    w_out,
    residual,
    norm_gain,
    w_router,
    routes,
    w_gate,
    w_up,
    w_down,
):
    y, x, z, core = (lax.axis_index(name) for name in ("y", "x", "z", "c"))
    ctx = (x * lax.axis_size("z") + z) * 2 + core
    requests = lengths.shape[0]
    features = query.shape[-1]
    width = w_out.shape[1]
    count = requests // 2
    cache = cache.swapaxes(1, 2)
    sibling_cache = shift_by(cache, "c", 1)
    own_query = query.reshape(requests, -1, features)
    stack_x = jnp.stack(all_shifts(own_query[:count], "x"))
    stack_z = jnp.stack(all_shifts(own_query[count:], "z"))
    queries_a = all_shifts(stack_x, "z")
    queries_b = all_shifts(stack_z, "x")
    blocks = jnp.stack([ctx, ctx ^ 1]).astype(jnp.int32)
    out_a = attend(blocks, lengths, queries_a, cache, sibling_cache, 0, count)
    out_b = attend(blocks, lengths, queries_b, cache, sibling_cache, count, count)
    final_a = return_shifts(merge(return_shifts(out_a, "z"), count), "x")
    final_b = return_shifts(merge(return_shifts(out_b, "x"), count), "z")
    kept, given = project(
        core.astype(jnp.int32).reshape(1), final_a, final_b, own_query, new_keys, value_up_weight, w_out, count
    )
    chip_sum = (kept.astype(f32) + shift_by(given, "c", 1).astype(f32)).astype(bf16)
    arrived = lax.all_to_all(chip_sum, ("x", "z"), split_axis=0, concat_axis=0, tiled=True)
    lanes = jnp.arange(LANES, dtype=jnp.int32)
    chosen = jnp.any(routes[:, :, None] == lanes[None, None, :], axis=1).astype(bf16)
    chosen = jnp.pad(chosen, ((0, SPAN - 1), (0, 0)))
    chips = lax.axis_size("y") * lax.axis_size("x") * lax.axis_size("z")
    attn_out, stream, rows = spread(
        arrived, residual.reshape(SPAN, -1), norm_gain.reshape(SPAN, -1), chosen, chips
    )
    own_rows = lax.all_to_all(rows, ("y", "x", "z"), split_axis=0, concat_axis=0, tiled=True)
    sibling_rows = shift_by(own_rows, "c", 1)
    devices = 2 * chips
    flat = y * (devices // lax.axis_size("y")) + ctx
    expert = (flat // (devices // EXPERTS)).astype(jnp.int32).reshape(1)
    out_own, out_sibling = experts(expert, own_rows, sibling_rows, w_gate, w_up, w_router, w_down)
    chip_out = (out_own.astype(f32) + shift_by(out_sibling, "c", 1).astype(f32)).astype(bf16)
    returned = lax.all_to_all(chip_out, ("y", "x", "z"), split_axis=0, concat_axis=0, tiled=True)
    layer_out = (stream.astype(f32) + jnp.sum(returned.astype(f32), axis=0)).astype(bf16)
    return (attn_out.reshape(1, width), layer_out.reshape(1, width))


def solution(mesh):
    names = ("y", "x", "z", "c")
    fine = Mesh(mesh.devices.reshape(4, 4, 4, 2), names)
    group, ctx = "y", ("x", "z", "c")
    return jax.shard_map(
        local,
        mesh=fine,
        in_specs=(
            P(group, ctx, None),
            P(group, ctx, None),
            P(group, None),
            P(group),
            P(ctx, None, None),
            P(ctx, None),
            P(names, None),
            P(),
            P(),
            P(names, None),
            P(None, names),
            P(None, names),
            P(names, None),
        ),
        out_specs=(P(names, None), P(names, None)),
        check_vma=False,
    )
```

```python
import functools

import jax
import jax.numpy as jnp
from jax import lax
from jax.experimental import pallas as pl
from jax.experimental.pallas import tpu as pltpu
from jax.sharding import Mesh, PartitionSpec as P

LATENT_WIDTH = 512
ROTARY_WIDTH = 64
QK_NOPE = 128
VALUE_HEAD_WIDTH = 128
EXPERTS = 16
LANES = 128
STAT = 16

neg_floor = -1e30
route_scale = 2.5
norm_eps = 1e-06
score_scale = (QK_NOPE + ROTARY_WIDTH) ** (-0.5)
f32 = jnp.float32
bf16 = jnp.bfloat16


def split3(value):
    high = value.astype(bf16).astype(f32)
    rest = value - high
    middle = rest.astype(bf16).astype(f32)
    return high, middle, (rest - middle).astype(bf16).astype(f32)


def place(stat_lanes, column, request, base):
    lane = lax.broadcasted_iota(jnp.int32, stat_lanes.shape, 1)
    for part, piece in enumerate(split3(column)):
        stat_lanes = jnp.where(lane == base + part * STAT + request, piece, stat_lanes)
    return stat_lanes


def join3(tile):
    return tile + pltpu.roll(tile, LANES - STAT, 1) + pltpu.roll(tile, LANES - 2 * STAT, 1)


def attend_kernel(blocks_ref, lengths_ref, q0, q1, q2, q3, own_ref, sib_ref, o0, o1, o2, o3, stat_ref, *, first, count):
    step = pl.program_id(0)
    length = lengths_ref[first + step]
    outs = (o0, o1, o2, o3)
    query = jnp.concatenate([ref[...].reshape(-1, ref.shape[-1]) for ref in (q0, q1, q2, q3)], axis=0)
    rows = query.shape[0]
    block_len = own_ref.shape[2]
    scores = []
    for which, keys in enumerate((own_ref, sib_ref)):
        score = score_scale * jnp.dot(query, keys[0], preferred_element_type=f32)
        position = blocks_ref[which] * block_len + lax.broadcasted_iota(jnp.int32, (1, block_len), 1)
        scores.append(jnp.where(position < length, score, neg_floor))
    top = jnp.maximum(
        jnp.max(scores[0], axis=-1, keepdims=True), jnp.max(scores[1], axis=-1, keepdims=True)
    )
    shift = jnp.where(top <= neg_floor, 0.0, top)
    total = jnp.zeros((rows, 1), f32)
    result = jnp.zeros((rows, LATENT_WIDTH), f32)
    for score, keys in zip(scores, (own_ref, sib_ref)):
        probability = jnp.exp(score - shift)
        total = total + jnp.sum(probability, axis=-1, keepdims=True)
        result = result + lax.dot_general(
            probability.astype(bf16),
            keys[0, :LATENT_WIDTH],
            (((1,), (1,)), ((), ())),
            preferred_element_type=f32,
        )

    @pl.when(step == 0)
    def _():
        stat_ref[...] = jnp.zeros_like(stat_ref)

    stats = place(place(stat_ref[...], top, step, 0), total, step, 3 * STAT)
    stat_ref[...] = stats
    part = rows // 4
    pieces = part // 16
    for d, out in enumerate(outs):
        for chunk in range(LATENT_WIDTH // LANES):
            tile = result[d * part : (d + 1) * part, chunk * LANES : (chunk + 1) * LANES]
            out[:, step * 4 + chunk] = tile.astype(bf16).reshape(pieces, 16, LANES)

    @pl.when(step == count - 1)
    def _():
        for d, out in enumerate(outs):
            out[:, 4 * count] = stats[d * part : (d + 1) * part].astype(bf16).reshape(pieces, 16, LANES)


def attend(blocks, lengths, queries, cache, sibling, first, count):
    features, block_len = cache.shape[1:]
    tiles = 4 * count + 1
    out = jax.ShapeDtypeStruct((4, tiles, 16, LANES), bf16)
    rows = 4 * queries[0].shape[0] * 16
    return pl.pallas_call(
        functools.partial(attend_kernel, first=first, count=count),
        out_shape=[out] * 4,
        grid_spec=pltpu.PrefetchScalarGridSpec(
            num_scalar_prefetch=2,
            grid=(count,),
            in_specs=[pl.BlockSpec((4, None, 16, features), lambda i, *_: (0, i, 0, 0))] * 4
            + [pl.BlockSpec((1, features, block_len), lambda i, *_: (first + i, 0, 0))] * 2,
            out_specs=[pl.BlockSpec((4, tiles, 16, LANES), lambda i, *_: (0, 0, 0, 0))] * 4,
            scratch_shapes=[pltpu.VMEM((rows, LANES), f32)],
        ),
        compiler_params=pltpu.CompilerParams(
            dimension_semantics=("arbitrary",), vmem_limit_bytes=48 << 20
        ),
        name="attend",
    )(blocks, lengths, *queries, cache, sibling)


def merged_stats(tiles):
    joined = [join3(tile) for tile in tiles]
    sums = [pltpu.roll(one, LANES - 3 * STAT, 1) for one in joined]
    top = functools.reduce(jnp.maximum, joined)
    weights = [jnp.exp(one - top) for one in joined]
    total = sum(weight * one for weight, one in zip(weights, sums))
    return weights, top, total


def merge_kernel(a0, a1, a2, a3, o0, o1, o2, o3, *, count):
    refs = (a0, a1, a2, a3)
    for piece, out in enumerate((o0, o1, o2, o3)):
        weights, top, total = merged_stats([ref[piece, 4 * count].astype(f32) for ref in refs])
        stats = jnp.zeros((16, LANES), f32)
        for request in range(count):
            stats = place(stats, top[:, request : request + 1], request, 0)
            stats = place(stats, total[:, request : request + 1], request, 3 * STAT)
            shares = [weight[:, request : request + 1] for weight in weights]
            for chunk in range(4):
                tile = sum(
                    share * ref[piece, 4 * request + chunk].astype(f32)
                    for share, ref in zip(shares, refs)
                )
                out[4 * request + chunk] = tile.astype(bf16)
        out[4 * count] = stats.astype(bf16)


def merge(pieces, count):
    return pl.pallas_call(
        functools.partial(merge_kernel, count=count),
        out_shape=[jax.ShapeDtypeStruct((4 * count + 1, 16, LANES), bf16)] * 4,
        compiler_params=pltpu.CompilerParams(vmem_limit_bytes=32 << 20),
        name="merge",
    )(*pieces)


def project_kernel(core_ref, *refs, count):
    first, second = refs[0:4], refs[4:8]
    q_ref, keys_ref, up_ref, w_hbm, kept_ref, given_ref, w_ref, rows_ref, sems = refs[8:]
    chunk = kept_ref.shape[2]

    def fetch(k):
        window = pl.ds(k * chunk, chunk)
        return pltpu.make_async_copy(w_hbm.at[:, window], w_ref.at[:, window], sems.at[k])

    for k in range(SPAN):
        fetch(k).start()
    tops, totals, results = [], [], []
    for half in (first, second):
        weights, top, total = merged_stats([ref[4 * count].astype(f32) for ref in half])
        for request in range(count):
            tops.append(top[:, request : request + 1])
            totals.append(total[:, request : request + 1])
            shares = [weight[:, request : request + 1] for weight in weights]
            results.append(
                jnp.concatenate(
                    [
                        sum(
                            share * ref[4 * request + part].astype(f32)
                            for share, ref in zip(shares, half)
                        )
                        for part in range(4)
                    ],
                    axis=1,
                )
            )
    cache_max = jnp.concatenate(tops, axis=0)
    cache_sum = jnp.concatenate(totals, axis=0)
    cache_result = jnp.concatenate(results, axis=0)
    rows = cache_max.shape[0]
    keys = keys_ref[...]
    near = score_scale * lax.dot_general(
        q_ref[...].reshape(rows, keys.shape[1]), keys, (((1,), (1,)), ((), ())), preferred_element_type=f32
    )
    row = lax.broadcasted_iota(jnp.int32, near.shape, 0)
    column = lax.broadcasted_iota(jnp.int32, near.shape, 1)
    seen = (row // 16 == column // 4) & (column % 4 <= (row % 16) // 4)
    near = jnp.where(seen, near, neg_floor)
    joint = jnp.maximum(cache_max, jnp.max(near, axis=-1, keepdims=True))
    rescale = jnp.exp(cache_max - joint)
    probability = jnp.where(seen, jnp.exp(near - joint), 0.0)
    denominator = cache_sum * rescale + jnp.sum(probability, axis=-1, keepdims=True)
    near_result = sum(
        jnp.dot(part.astype(bf16), keys[:, :LATENT_WIDTH], preferred_element_type=f32)
        for part in split3(probability)
    )
    latent = ((cache_result * rescale + near_result) / denominator).astype(bf16)
    grouped = rows // 4
    pick_row = lax.broadcasted_iota(jnp.int32, (grouped, rows), 0)
    pick_column = lax.broadcasted_iota(jnp.int32, (grouped, rows), 1)
    halves = grouped // 2
    core = core_ref[0]
    order = 2 * (pick_row % halves) + jnp.where(pick_row < halves, core, 1 - core)
    values = []
    for head in range(4):
        head_value = jnp.dot(latent, up_ref[head], preferred_element_type=f32).astype(bf16)
        pick = (pick_column == 4 * order + head).astype(f32).astype(bf16)
        values.append(jnp.dot(pick, head_value, preferred_element_type=f32).astype(bf16))
    values = jnp.concatenate(values, axis=1)
    for k in range(SPAN):
        fetch(k).wait()
        block = jnp.dot(values, w_ref[:, k * chunk : (k + 1) * chunk], preferred_element_type=f32)
        for piece in range(chunk // LANES):
            rows_ref[piece, pl.ds(k, grouped, stride=SPAN), :] = block[:, piece * LANES : (piece + 1) * LANES]
    for piece in range(chunk // LANES):
        window = slice(piece * LANES, (piece + 1) * LANES)
        whole = rows_ref[piece].reshape(grouped, SPAN, LANES).astype(bf16)
        kept_ref[:, :, window] = whole[:halves]
        given_ref[:, :, window] = whole[halves:]


SPAN = 8


def project(core, first, second, own_query, new_keys, value_up, w_out, count):
    grouped = new_keys.shape[0]
    width = w_out.shape[1]
    out = jax.ShapeDtypeStruct((grouped // 2, SPAN, width // SPAN), bf16)
    inside = pl.BlockSpec(memory_space=pltpu.VMEM)
    return pl.pallas_call(
        functools.partial(project_kernel, count=count),
        out_shape=[out, out],
        in_specs=[pl.BlockSpec(memory_space=pltpu.SMEM)] + [inside] * 11 + [pl.BlockSpec(memory_space=pltpu.HBM)],
        out_specs=[inside] * 2,
        scratch_shapes=[
            pltpu.VMEM(w_out.shape, bf16),
            pltpu.VMEM((width // SPAN // LANES, grouped * SPAN, LANES), f32),
            pltpu.SemaphoreType.DMA((SPAN,)),
        ],
        compiler_params=pltpu.CompilerParams(vmem_limit_bytes=32 << 20),
        name="project",
    )(core, *first, *second, own_query, new_keys, value_up, pltpu.with_memory_space_constraint(w_out, pltpu.HBM))


def spread_kernel(arrived_ref, residual_ref, gain_ref, attn_ref, stream_ref, normed_ref, rows_ref):
    attention = jnp.sum(arrived_ref[...].astype(f32), axis=0)
    attn_ref[...] = attention.astype(bf16)
    stream = (residual_ref[...].astype(f32) + attention).astype(bf16)
    stream_ref[...] = stream
    wide = stream.astype(f32)
    square = jnp.sum(jnp.sum(wide * wide, axis=1, keepdims=True), axis=0, keepdims=True)
    mean_square = square / (wide.shape[0] * wide.shape[1])
    normed = (wide * lax.rsqrt(mean_square + norm_eps) * gain_ref[...]).astype(bf16)
    normed_ref[...] = normed
    rows_ref[...] = jnp.broadcast_to(normed[None], rows_ref.shape)


def spread(arrived, residual, gain, chips):
    one = jax.ShapeDtypeStruct(residual.shape, bf16)
    rows = jax.ShapeDtypeStruct((chips,) + residual.shape, bf16)
    return pl.pallas_call(
        spread_kernel,
        out_shape=[one, one, one, rows],
        compiler_params=pltpu.CompilerParams(vmem_limit_bytes=32 << 20),
        name="spread",
    )(arrived, residual, gain)


def experts_kernel(
    routes_ref, own_ref, sib_ref, normed_ref, router_ref, gate_hbm, up_hbm, down_hbm,
    out_own, out_sib, coefficient_ref, gate_ref, up_ref, down_ref, rows_ref, sems
):
    half = own_ref.shape[0]
    rows = 2 * half
    chunk = out_own.shape[2]
    tiles = chunk // LANES

    def fetch(which, k):
        window = pl.ds(k * chunk, chunk)
        source, target = ((gate_hbm, gate_ref), (up_hbm, up_ref), (down_hbm, down_ref))[which]
        if which == 2:
            return pltpu.make_async_copy(source.at[:, window], target.at[:, window], sems.at[which, k])
        return pltpu.make_async_copy(source.at[window], target.at[window], sems.at[which, k])

    for k in range(SPAN):
        fetch(0, k).start()
        fetch(1, k).start()
    for k in range(SPAN):
        fetch(2, k).start()
    for piece in range(tiles):
        window = slice(piece * LANES, (piece + 1) * LANES)
        rows_ref[piece, : half * SPAN] = own_ref[:, :, window].astype(f32).reshape(half * SPAN, LANES)
        rows_ref[piece, half * SPAN :] = sib_ref[:, :, window].astype(f32).reshape(half * SPAN, LANES)
    products = router_ref[...].astype(f32) * normed_ref[...].astype(f32)[None]
    values = jnp.sum(jnp.sum(products, axis=2, keepdims=True), axis=1, keepdims=True)
    values = 1.0 / (1.0 + jnp.exp(-values))
    index = lax.broadcasted_iota(jnp.int32, values.shape, 0)
    chosen = jnp.zeros(values.shape, f32)
    for k in range(routes_ref.shape[1]):
        chosen = jnp.where(index == routes_ref[0, k], 1.0, chosen)
    picked = values * chosen
    share = route_scale * picked / jnp.sum(picked, axis=0, keepdims=True)
    coefficient_ref[...] = jnp.broadcast_to(share, coefficient_ref.shape)
    gate = up = 0.0
    for k in range(SPAN):
        block = jnp.concatenate(
            [rows_ref[piece, pl.ds(k, rows, stride=SPAN), :] for piece in range(tiles)], axis=1
        ).astype(bf16)
        fetch(0, k).wait()
        gate = gate + jnp.dot(block, gate_ref[k * chunk : (k + 1) * chunk], preferred_element_type=f32)
        fetch(1, k).wait()
        up = up + jnp.dot(block, up_ref[k * chunk : (k + 1) * chunk], preferred_element_type=f32)
    hidden = (gate / (1.0 + jnp.exp(-gate)) * up).astype(bf16)
    for k in range(SPAN):
        fetch(2, k).wait()
        result = jnp.dot(hidden, down_ref[:, k * chunk : (k + 1) * chunk], preferred_element_type=f32)
        for piece in range(tiles):
            rows_ref[piece, pl.ds(k, rows, stride=SPAN), :] = result[:, piece * LANES : (piece + 1) * LANES]
    for piece in range(tiles):
        window = slice(piece * LANES, (piece + 1) * LANES)
        out_own[:, :, window] = rows_ref[piece, : half * SPAN].reshape(half, SPAN, LANES).astype(bf16)
        out_sib[:, :, window] = rows_ref[piece, half * SPAN :].reshape(half, SPAN, LANES).astype(bf16)


def experts(routes, own_rows, sibling_rows, normed, w_router, w_gate, w_up, w_down):
    out = jax.ShapeDtypeStruct(own_rows.shape, bf16)
    inside = pl.BlockSpec(memory_space=pltpu.VMEM)
    outside = pl.BlockSpec(memory_space=pltpu.HBM)
    half, span, chunk = own_rows.shape
    weights = [pltpu.with_memory_space_constraint(w, pltpu.HBM) for w in (w_gate, w_up, w_down)]
    return pl.pallas_call(
        experts_kernel,
        out_shape=[out, out, jax.ShapeDtypeStruct((EXPERTS, span, LANES), f32)],
        in_specs=[pl.BlockSpec(memory_space=pltpu.SMEM)] + [inside] * 4 + [outside] * 3,
        out_specs=[inside] * 3,
        scratch_shapes=[
            pltpu.VMEM(w_gate.shape, bf16),
            pltpu.VMEM(w_up.shape, bf16),
            pltpu.VMEM(w_down.shape, bf16),
            pltpu.VMEM((chunk // LANES, 2 * half * span, LANES), f32),
            pltpu.SemaphoreType.DMA((3, span)),
        ],
        compiler_params=pltpu.CompilerParams(vmem_limit_bytes=48 << 20),
        name="experts",
    )(routes, own_rows, sibling_rows, normed, w_router.T.reshape(EXPERTS, span, chunk), *weights)


def gather_kernel(returned_ref, stream_ref, coefficient_ref, out_ref):
    slices = returned_ref.shape[0] // EXPERTS
    for piece in range(stream_ref.shape[1] // LANES):
        window = slice(piece * LANES, (piece + 1) * LANES)
        total = jnp.zeros((SPAN, LANES), f32)
        for expert in range(EXPERTS):
            part = returned_ref[expert * slices : (expert + 1) * slices, :, window].astype(f32)
            total = total + coefficient_ref[expert] * jnp.sum(part, axis=0)
        out_ref[:, window] = (stream_ref[:, window].astype(f32) + total).astype(bf16)


def gather(returned, stream, coefficient):
    return pl.pallas_call(
        gather_kernel,
        out_shape=jax.ShapeDtypeStruct(stream.shape, bf16),
        compiler_params=pltpu.CompilerParams(vmem_limit_bytes=32 << 20),
        name="gather",
    )(returned, stream, coefficient)


def shift_by(value, axis, offset):
    size = lax.axis_size(axis)
    return lax.ppermute(value, axis, [(i, (i + offset) % size) for i in range(size)])


def all_shifts(value, axis):
    return [value] + [shift_by(value, axis, d) for d in range(1, lax.axis_size(axis))]


def return_shifts(pieces, axis):
    return [pieces[0]] + [shift_by(piece, axis, -d) for d, piece in enumerate(pieces) if d > 0]


def local(
    query,
    cache,
    new_keys,
    lengths,
    value_up_weight,
    w_out,
    residual,
    norm_gain,
    w_router,
    routes,
    w_gate,
    w_up,
    w_down,
):
    x, z, core = (lax.axis_index(name) for name in ("x", "z", "c"))
    ctx = (x * lax.axis_size("z") + z) * 2 + core
    requests = lengths.shape[0]
    features = query.shape[-1]
    width = w_out.shape[1]
    count = requests // 2
    cache = cache.swapaxes(1, 2)
    sibling_cache = shift_by(cache, "c", 1)
    own_query = query.reshape(requests, -1, features)
    stack_x = jnp.stack(all_shifts(own_query[:count], "x"))
    stack_z = jnp.stack(all_shifts(own_query[count:], "z"))
    stack_x, stack_z = lax.optimization_barrier((stack_x, stack_z))
    queries_a = all_shifts(stack_x, "z")
    queries_b = all_shifts(stack_z, "x")
    blocks = jnp.stack([ctx, ctx ^ 1]).astype(jnp.int32)
    out_a = attend(blocks, lengths, queries_a, cache, sibling_cache, 0, count)
    out_b = attend(blocks, lengths, queries_b, cache, sibling_cache, count, count)
    final_a = return_shifts(merge(return_shifts(out_a, "z"), count), "x")
    final_b = return_shifts(merge(return_shifts(out_b, "x"), count), "z")
    kept, given = project(
        core.astype(jnp.int32).reshape(1), final_a, final_b, own_query, new_keys, value_up_weight, w_out, count
    )
    chip_sum = (kept.astype(f32) + shift_by(given, "c", 1).astype(f32)).astype(bf16)
    arrived = lax.all_to_all(chip_sum, ("x", "z"), split_axis=0, concat_axis=0, tiled=True)
    chips = lax.axis_size("y") * lax.axis_size("x") * lax.axis_size("z")
    attn_out, stream, normed, rows = spread(
        arrived, residual.reshape(SPAN, -1), norm_gain.reshape(SPAN, -1), chips
    )
    own_rows = lax.all_to_all(rows, ("y", "x", "z"), split_axis=0, concat_axis=0, tiled=True)
    sibling_rows = shift_by(own_rows, "c", 1)
    out_own, out_sibling, coefficient = experts(
        routes, own_rows, sibling_rows, normed, w_router, w_gate, w_up, w_down
    )
    chip_out = (out_own.astype(f32) + shift_by(out_sibling, "c", 1).astype(f32)).astype(bf16)
    returned = lax.all_to_all(chip_out, ("y", "x", "z"), split_axis=0, concat_axis=0, tiled=True)
    layer_out = gather(returned, stream, coefficient)
    return (attn_out.reshape(1, width), layer_out.reshape(1, width))


def solution(mesh):
    names = ("y", "x", "z", "c")
    fine = Mesh(mesh.devices.reshape(4, 4, 4, 2), names)
    group, ctx = "y", ("x", "z", "c")
    return jax.shard_map(
        local,
        mesh=fine,
        in_specs=(
            P(group, ctx, None),
            P(group, ctx, None),
            P(group, None),
            P(group),
            P(ctx, None, None),
            P(ctx, None),
            P(names, None),
            P(),
            P(),
            P(names, None),
            P(None, names),
            P(None, names),
            P(names, None),
        ),
        out_specs=(P(names, None), P(names, None)),
        check_vma=False,
    )
```

```python
import functools

import jax
import jax.numpy as jnp
from jax import lax
from jax.experimental import pallas as pl
from jax.experimental.pallas import tpu as pltpu
from jax.sharding import Mesh, PartitionSpec as P

LATENT_WIDTH = 512
ROTARY_WIDTH = 64
QK_NOPE = 128
VALUE_HEAD_WIDTH = 128
EXPERTS = 16
LANES = 128
STAT = 16

neg_floor = -1e30
route_scale = 2.5
norm_eps = 1e-06
score_scale = (QK_NOPE + ROTARY_WIDTH) ** (-0.5)
f32 = jnp.float32
bf16 = jnp.bfloat16


def split3(value):
    high = value.astype(bf16).astype(f32)
    rest = value - high
    middle = rest.astype(bf16).astype(f32)
    return high, middle, (rest - middle).astype(bf16).astype(f32)


def place(stat_lanes, column, request, base):
    lane = lax.broadcasted_iota(jnp.int32, stat_lanes.shape, 1)
    for part, piece in enumerate(split3(column)):
        stat_lanes = jnp.where(lane == base + part * STAT + request, piece, stat_lanes)
    return stat_lanes


def join3(tile):
    return tile + pltpu.roll(tile, LANES - STAT, 1) + pltpu.roll(tile, LANES - 2 * STAT, 1)


def attend_kernel(scalars_ref, q0, q1, q2, q3, own_ref, sib_ref, o0, o1, o2, o3, stat_ref, *, first, count):
    step = pl.program_id(0)
    length = scalars_ref[2 + first + step]
    outs = (o0, o1, o2, o3)
    query = jnp.concatenate([ref[...].reshape(-1, ref.shape[-1]) for ref in (q0, q1, q2, q3)], axis=0)
    rows = query.shape[0]
    block_len = own_ref.shape[2]
    scores = []
    for which, keys in enumerate((own_ref, sib_ref)):
        score = score_scale * jnp.dot(query, keys[0], preferred_element_type=f32)
        position = scalars_ref[which] * block_len + lax.broadcasted_iota(jnp.int32, (1, block_len), 1)
        scores.append(jnp.where(position < length, score, neg_floor))
    top = jnp.maximum(
        jnp.max(scores[0], axis=-1, keepdims=True), jnp.max(scores[1], axis=-1, keepdims=True)
    )
    shift = jnp.where(top <= neg_floor, 0.0, top)
    total = jnp.zeros((rows, 1), f32)
    result = jnp.zeros((rows, LATENT_WIDTH), f32)
    for score, keys in zip(scores, (own_ref, sib_ref)):
        probability = jnp.exp(score - shift)
        total = total + jnp.sum(probability, axis=-1, keepdims=True)
        result = result + lax.dot_general(
            probability.astype(bf16),
            keys[0, :LATENT_WIDTH],
            (((1,), (1,)), ((), ())),
            preferred_element_type=f32,
        )

    @pl.when(step == 0)
    def _():
        stat_ref[...] = jnp.zeros_like(stat_ref)

    stats = place(place(stat_ref[...], top, step, 0), total, step, 3 * STAT)
    stat_ref[...] = stats
    part = rows // 4
    pieces = part // 16
    for d, out in enumerate(outs):
        for chunk in range(LATENT_WIDTH // LANES):
            tile = result[d * part : (d + 1) * part, chunk * LANES : (chunk + 1) * LANES]
            out[:, step * 4 + chunk] = tile.astype(bf16).reshape(pieces, 16, LANES)

    @pl.when(step == count - 1)
    def _():
        for d, out in enumerate(outs):
            out[:, 4 * count] = stats[d * part : (d + 1) * part].astype(bf16).reshape(pieces, 16, LANES)


def attend(scalars, queries, cache, sibling, first, count):
    features, block_len = cache.shape[1:]
    tiles = 4 * count + 1
    out = jax.ShapeDtypeStruct((4, tiles, 16, LANES), bf16)
    rows = 4 * queries[0].shape[0] * 16
    return pl.pallas_call(
        functools.partial(attend_kernel, first=first, count=count),
        out_shape=[out] * 4,
        grid_spec=pltpu.PrefetchScalarGridSpec(
            num_scalar_prefetch=1,
            grid=(count,),
            in_specs=[pl.BlockSpec((4, None, 16, features), lambda i, *_: (0, i, 0, 0))] * 4
            + [pl.BlockSpec((1, features, block_len), lambda i, *_: (first + i, 0, 0))] * 2,
            out_specs=[pl.BlockSpec((4, tiles, 16, LANES), lambda i, *_: (0, 0, 0, 0))] * 4,
            scratch_shapes=[pltpu.VMEM((rows, LANES), f32)],
        ),
        compiler_params=pltpu.CompilerParams(
            dimension_semantics=("arbitrary",), vmem_limit_bytes=48 << 20
        ),
        name="attend",
    )(scalars, *queries, cache, sibling)


def merged_stats(tiles):
    joined = [join3(tile) for tile in tiles]
    sums = [pltpu.roll(one, LANES - 3 * STAT, 1) for one in joined]
    top = functools.reduce(jnp.maximum, joined)
    weights = [jnp.exp(one - top) for one in joined]
    total = sum(weight * one for weight, one in zip(weights, sums))
    return weights, top, total


def merge_kernel(a0, a1, a2, a3, o0, o1, o2, o3, *, count):
    refs = (a0, a1, a2, a3)
    for piece, out in enumerate((o0, o1, o2, o3)):
        weights, top, total = merged_stats([ref[piece, 4 * count].astype(f32) for ref in refs])
        stats = jnp.zeros((16, LANES), f32)
        for request in range(count):
            stats = place(stats, top[:, request : request + 1], request, 0)
            stats = place(stats, total[:, request : request + 1], request, 3 * STAT)
            shares = [weight[:, request : request + 1] for weight in weights]
            for chunk in range(4):
                tile = sum(
                    share * ref[piece, 4 * request + chunk].astype(f32)
                    for share, ref in zip(shares, refs)
                )
                out[4 * request + chunk] = tile.astype(bf16)
        out[4 * count] = stats.astype(bf16)


def merge(pieces, count):
    return pl.pallas_call(
        functools.partial(merge_kernel, count=count),
        out_shape=[jax.ShapeDtypeStruct((4 * count + 1, 16, LANES), bf16)] * 4,
        compiler_params=pltpu.CompilerParams(vmem_limit_bytes=32 << 20),
        name="merge",
    )(*pieces)


def project_kernel(core_ref, *refs, count):
    first, second = refs[0:4], refs[4:8]
    q_ref, keys_ref, up_ref, w_hbm, kept_ref, given_ref, w_ref, rows_ref, sems = refs[8:]
    chunk = kept_ref.shape[2]

    def fetch(k):
        window = pl.ds(k * chunk, chunk)
        return pltpu.make_async_copy(w_hbm.at[:, window], w_ref.at[:, window], sems.at[k])

    for k in range(SPAN):
        fetch(k).start()
    tops, totals, results = [], [], []
    for half in (first, second):
        weights, top, total = merged_stats([ref[4 * count].astype(f32) for ref in half])
        for request in range(count):
            tops.append(top[:, request : request + 1])
            totals.append(total[:, request : request + 1])
            shares = [weight[:, request : request + 1] for weight in weights]
            results.append(
                jnp.concatenate(
                    [
                        sum(
                            share * ref[4 * request + part].astype(f32)
                            for share, ref in zip(shares, half)
                        )
                        for part in range(4)
                    ],
                    axis=1,
                )
            )
    cache_max = jnp.concatenate(tops, axis=0)
    cache_sum = jnp.concatenate(totals, axis=0)
    cache_result = jnp.concatenate(results, axis=0)
    rows = cache_max.shape[0]
    keys = keys_ref[...]
    near = score_scale * lax.dot_general(
        q_ref[...].reshape(rows, keys.shape[1]), keys, (((1,), (1,)), ((), ())), preferred_element_type=f32
    )
    row = lax.broadcasted_iota(jnp.int32, near.shape, 0)
    column = lax.broadcasted_iota(jnp.int32, near.shape, 1)
    seen = (row // 16 == column // 4) & (column % 4 <= (row % 16) // 4)
    near = jnp.where(seen, near, neg_floor)
    joint = jnp.maximum(cache_max, jnp.max(near, axis=-1, keepdims=True))
    rescale = jnp.exp(cache_max - joint)
    probability = jnp.where(seen, jnp.exp(near - joint), 0.0)
    denominator = cache_sum * rescale + jnp.sum(probability, axis=-1, keepdims=True)
    near_result = sum(
        jnp.dot(part.astype(bf16), keys[:, :LATENT_WIDTH], preferred_element_type=f32)
        for part in split3(probability)
    )
    latent = ((cache_result * rescale + near_result) / denominator).astype(bf16)
    grouped = rows // 4
    pick_row = lax.broadcasted_iota(jnp.int32, (grouped, rows), 0)
    pick_column = lax.broadcasted_iota(jnp.int32, (grouped, rows), 1)
    halves = grouped // 2
    core = core_ref[0]
    order = 2 * (pick_row % halves) + jnp.where(pick_row < halves, core, 1 - core)
    values = []
    for head in range(4):
        head_value = jnp.dot(latent, up_ref[head], preferred_element_type=f32).astype(bf16)
        pick = (pick_column == 4 * order + head).astype(f32).astype(bf16)
        values.append(jnp.dot(pick, head_value, preferred_element_type=f32).astype(bf16))
    values = jnp.concatenate(values, axis=1)
    for k in range(SPAN):
        fetch(k).wait()
        block = jnp.dot(values, w_ref[:, k * chunk : (k + 1) * chunk], preferred_element_type=f32)
        for piece in range(chunk // LANES):
            rows_ref[piece, pl.ds(k, grouped, stride=SPAN), :] = block[:, piece * LANES : (piece + 1) * LANES]
    for piece in range(chunk // LANES):
        window = slice(piece * LANES, (piece + 1) * LANES)
        whole = rows_ref[piece].reshape(grouped, SPAN, LANES).astype(bf16)
        kept_ref[:, :, window] = whole[:halves]
        given_ref[:, :, window] = whole[halves:]


SPAN = 8


def project(core, first, second, own_query, new_keys, value_up, w_out, count):
    grouped = new_keys.shape[0]
    width = w_out.shape[1]
    out = jax.ShapeDtypeStruct((grouped // 2, SPAN, width // SPAN), bf16)
    inside = pl.BlockSpec(memory_space=pltpu.VMEM)
    return pl.pallas_call(
        functools.partial(project_kernel, count=count),
        out_shape=[out, out],
        in_specs=[pl.BlockSpec(memory_space=pltpu.SMEM)] + [inside] * 11 + [pl.BlockSpec(memory_space=pltpu.HBM)],
        out_specs=[inside] * 2,
        scratch_shapes=[
            pltpu.VMEM(w_out.shape, bf16),
            pltpu.VMEM((width // SPAN // LANES, grouped * SPAN, LANES), f32),
            pltpu.SemaphoreType.DMA((SPAN,)),
        ],
        compiler_params=pltpu.CompilerParams(vmem_limit_bytes=32 << 20),
        name="project",
    )(core, *first, *second, own_query, new_keys, value_up, pltpu.with_memory_space_constraint(w_out, pltpu.HBM))


def spread_kernel(arrived_ref, residual_ref, gain_ref, attn_ref, stream_ref, normed_ref, rows_ref):
    attention = jnp.sum(arrived_ref[...].astype(f32), axis=0)
    attn_ref[...] = attention.astype(bf16)
    stream = (residual_ref[...].astype(f32) + attention).astype(bf16)
    stream_ref[...] = stream
    wide = stream.astype(f32)
    square = jnp.sum(jnp.sum(wide * wide, axis=1, keepdims=True), axis=0, keepdims=True)
    mean_square = square / (wide.shape[0] * wide.shape[1])
    normed = (wide * lax.rsqrt(mean_square + norm_eps) * gain_ref[...]).astype(bf16)
    normed_ref[...] = normed
    rows_ref[...] = jnp.broadcast_to(normed[None], rows_ref.shape)


def spread(arrived, residual, gain, chips):
    one = jax.ShapeDtypeStruct(residual.shape, bf16)
    rows = jax.ShapeDtypeStruct((chips,) + residual.shape, bf16)
    return pl.pallas_call(
        spread_kernel,
        out_shape=[one, one, one, rows],
        compiler_params=pltpu.CompilerParams(vmem_limit_bytes=32 << 20),
        name="spread",
    )(arrived, residual, gain)


def route_kernel(routes_ref, normed_ref, router_ref, coefficient_ref):
    products = router_ref[...].astype(f32) * normed_ref[...].astype(f32)[None]
    values = jnp.sum(jnp.sum(products, axis=2, keepdims=True), axis=1, keepdims=True)
    values = 1.0 / (1.0 + jnp.exp(-values))
    index = lax.broadcasted_iota(jnp.int32, values.shape, 0)
    chosen = jnp.zeros(values.shape, f32)
    for k in range(routes_ref.shape[1]):
        chosen = jnp.where(index == routes_ref[0, k], 1.0, chosen)
    picked = values * chosen
    share = route_scale * picked / jnp.sum(picked, axis=0, keepdims=True)
    coefficient_ref[...] = jnp.broadcast_to(share, coefficient_ref.shape)


def route(routes, normed, w_router):
    span, chunk = normed.shape
    inside = pl.BlockSpec(memory_space=pltpu.VMEM)
    return pl.pallas_call(
        route_kernel,
        out_shape=jax.ShapeDtypeStruct((EXPERTS, span, LANES), f32),
        in_specs=[pl.BlockSpec(memory_space=pltpu.SMEM), inside, inside],
        compiler_params=pltpu.CompilerParams(vmem_limit_bytes=16 << 20),
        name="route",
    )(routes, normed, w_router.T.reshape(EXPERTS, span, chunk))


def hold_kernel(*refs):
    count = len(refs) // 2
    sems = refs[-1]
    copies = []
    for i, (source, target) in enumerate(zip(refs[:count], refs[count : 2 * count])):
        part = source.shape[0] // SPAN
        for k in range(SPAN):
            window = pl.ds(k * part, part)
            copies.append(pltpu.make_async_copy(source.at[window], target.at[window], sems.at[i, k]))
    for copy in copies:
        copy.start()
    for copy in copies:
        copy.wait()


def hold(*weights):
    return pl.pallas_call(
        hold_kernel,
        out_shape=[pltpu.VMEM(w.shape, w.dtype) for w in weights],
        in_specs=[pl.BlockSpec(memory_space=pltpu.HBM)] * len(weights),
        out_specs=[pl.BlockSpec(memory_space=pltpu.VMEM)] * len(weights),
        scratch_shapes=[pltpu.SemaphoreType.DMA((len(weights), SPAN))],
        compiler_params=pltpu.CompilerParams(vmem_limit_bytes=24 << 20),
        name="hold",
    )(*[pltpu.with_memory_space_constraint(w, pltpu.HBM) for w in weights])


def experts_kernel(own_ref, sib_ref, gate_ref, up_ref, down_hbm, out_own, out_sib, down_ref, rows_ref, sems):
    half = own_ref.shape[0]
    rows = 2 * half
    chunk = out_own.shape[2]
    tiles = chunk // LANES

    def fetch(k):
        window = pl.ds(k * chunk, chunk)
        return pltpu.make_async_copy(down_hbm.at[:, window], down_ref.at[:, window], sems.at[k])

    for k in range(SPAN):
        fetch(k).start()
    for piece in range(tiles):
        window = slice(piece * LANES, (piece + 1) * LANES)
        rows_ref[piece, : half * SPAN] = own_ref[:, :, window].astype(f32).reshape(half * SPAN, LANES)
        rows_ref[piece, half * SPAN :] = sib_ref[:, :, window].astype(f32).reshape(half * SPAN, LANES)
    gate = up = 0.0
    for k in range(SPAN):
        block = jnp.concatenate(
            [rows_ref[piece, pl.ds(k, rows, stride=SPAN), :] for piece in range(tiles)], axis=1
        ).astype(bf16)
        gate = gate + jnp.dot(block, gate_ref[k * chunk : (k + 1) * chunk], preferred_element_type=f32)
        up = up + jnp.dot(block, up_ref[k * chunk : (k + 1) * chunk], preferred_element_type=f32)
    hidden = (gate / (1.0 + jnp.exp(-gate)) * up).astype(bf16)
    for k in range(SPAN):
        fetch(k).wait()
        result = jnp.dot(hidden, down_ref[:, k * chunk : (k + 1) * chunk], preferred_element_type=f32)
        for piece in range(tiles):
            rows_ref[piece, pl.ds(k, rows, stride=SPAN), :] = result[:, piece * LANES : (piece + 1) * LANES]
    for piece in range(tiles):
        window = slice(piece * LANES, (piece + 1) * LANES)
        out_own[:, :, window] = rows_ref[piece, : half * SPAN].reshape(half, SPAN, LANES).astype(bf16)
        out_sib[:, :, window] = rows_ref[piece, half * SPAN :].reshape(half, SPAN, LANES).astype(bf16)


def experts(own_rows, sibling_rows, w_gate, w_up, w_down):
    out = jax.ShapeDtypeStruct(own_rows.shape, bf16)
    inside = pl.BlockSpec(memory_space=pltpu.VMEM)
    half, span, chunk = own_rows.shape
    return pl.pallas_call(
        experts_kernel,
        out_shape=[out, out],
        in_specs=[inside] * 4 + [pl.BlockSpec(memory_space=pltpu.HBM)],
        out_specs=[inside] * 2,
        scratch_shapes=[
            pltpu.VMEM(w_down.shape, bf16),
            pltpu.VMEM((chunk // LANES, 2 * half * span, LANES), f32),
            pltpu.SemaphoreType.DMA((span,)),
        ],
        compiler_params=pltpu.CompilerParams(vmem_limit_bytes=20 << 20),
        name="experts",
    )(own_rows, sibling_rows, w_gate, w_up, pltpu.with_memory_space_constraint(w_down, pltpu.HBM))


def gather_kernel(returned_ref, stream_ref, coefficient_ref, out_ref):
    slices = returned_ref.shape[0] // EXPERTS
    for piece in range(stream_ref.shape[1] // LANES):
        window = slice(piece * LANES, (piece + 1) * LANES)
        total = jnp.zeros((SPAN, LANES), f32)
        for expert in range(EXPERTS):
            part = returned_ref[expert * slices : (expert + 1) * slices, :, window].astype(f32)
            total = total + coefficient_ref[expert] * jnp.sum(part, axis=0)
        out_ref[:, window] = (stream_ref[:, window].astype(f32) + total).astype(bf16)


def gather(returned, stream, coefficient):
    return pl.pallas_call(
        gather_kernel,
        out_shape=jax.ShapeDtypeStruct(stream.shape, bf16),
        compiler_params=pltpu.CompilerParams(vmem_limit_bytes=32 << 20),
        name="gather",
    )(returned, stream, coefficient)


def shift_by(value, axis, offset):
    size = lax.axis_size(axis)
    return lax.ppermute(value, axis, [(i, (i + offset) % size) for i in range(size)])


def all_shifts(value, axis):
    return [value] + [shift_by(value, axis, d) for d in range(1, lax.axis_size(axis))]


def return_shifts(pieces, axis):
    return [pieces[0]] + [shift_by(piece, axis, -d) for d, piece in enumerate(pieces) if d > 0]


def local(
    query,
    cache,
    new_keys,
    lengths,
    value_up_weight,
    w_out,
    residual,
    norm_gain,
    w_router,
    routes,
    w_gate,
    w_up,
    w_down,
):
    x, z, core = (lax.axis_index(name) for name in ("x", "z", "c"))
    ctx = (x * lax.axis_size("z") + z) * 2 + core
    requests = lengths.shape[0]
    features = query.shape[-1]
    width = w_out.shape[1]
    count = requests // 2
    cache = cache.swapaxes(1, 2)
    sibling_cache = shift_by(cache, "c", 1)
    own_query = query.reshape(requests, -1, features)
    stack_x = jnp.stack(all_shifts(own_query[:count], "x"))
    stack_z = jnp.stack(all_shifts(own_query[count:], "z"))
    stack_x, stack_z = lax.optimization_barrier((stack_x, stack_z))
    queries_a = all_shifts(stack_x, "z")
    queries_b = all_shifts(stack_z, "x")
    scalars = jnp.concatenate([jnp.stack([ctx, ctx ^ 1]).astype(jnp.int32), lengths])
    out_a = attend(scalars, queries_a, cache, sibling_cache, 0, count)
    out_b = attend(scalars, queries_b, cache, sibling_cache, count, count)
    final_a = return_shifts(merge(return_shifts(out_a, "z"), count), "x")
    final_b = return_shifts(merge(return_shifts(out_b, "x"), count), "z")
    kept, given = project(
        core.astype(jnp.int32).reshape(1), final_a, final_b, own_query, new_keys, value_up_weight, w_out, count
    )
    chip_sum = (kept.astype(f32) + shift_by(given, "c", 1).astype(f32)).astype(bf16)
    arrived = lax.all_to_all(chip_sum, ("x", "z"), split_axis=0, concat_axis=0, tiled=True)
    chips = lax.axis_size("y") * lax.axis_size("x") * lax.axis_size("z")
    attn_out, stream, normed, rows = spread(
        arrived, residual.reshape(SPAN, -1), norm_gain.reshape(SPAN, -1), chips
    )
    normed, *weights = lax.optimization_barrier((normed, w_gate, w_up))
    weights = hold(*weights)
    coefficient = route(routes, normed, w_router)
    own_rows = lax.all_to_all(rows, ("y", "x", "z"), split_axis=0, concat_axis=0, tiled=True)
    own_rows, coefficient = lax.optimization_barrier((own_rows, coefficient))
    sibling_rows = shift_by(own_rows, "c", 1)
    out_own, out_sibling = experts(own_rows, sibling_rows, *weights, w_down)
    chip_out = (out_own.astype(f32) + shift_by(out_sibling, "c", 1).astype(f32)).astype(bf16)
    returned = lax.all_to_all(chip_out, ("y", "x", "z"), split_axis=0, concat_axis=0, tiled=True)
    layer_out = gather(returned, stream, coefficient)
    return (attn_out.reshape(1, width), layer_out.reshape(1, width))


def solution(mesh):
    names = ("y", "x", "z", "c")
    fine = Mesh(mesh.devices.reshape(4, 4, 4, 2), names)
    group, ctx = "y", ("x", "z", "c")
    return jax.shard_map(
        local,
        mesh=fine,
        in_specs=(
            P(group, ctx, None),
            P(group, ctx, None),
            P(group, None),
            P(group),
            P(ctx, None, None),
            P(ctx, None),
            P(names, None),
            P(),
            P(),
            P(names, None),
            P(None, names),
            P(None, names),
            P(names, None),
        ),
        out_specs=(P(names, None), P(names, None)),
        check_vma=False,
    )
```

```python
import functools

import jax
import jax.numpy as jnp
from jax import lax
from jax.experimental import pallas as pl
from jax.experimental.pallas import tpu as pltpu
from jax.sharding import Mesh, PartitionSpec as P

LATENT_WIDTH = 512
ROTARY_WIDTH = 64
QK_NOPE = 128
VALUE_HEAD_WIDTH = 128
EXPERTS = 16
LANES = 128
STAT = 16

neg_floor = -1e30
route_scale = 2.5
norm_eps = 1e-06
score_scale = (QK_NOPE + ROTARY_WIDTH) ** (-0.5)
f32 = jnp.float32
bf16 = jnp.bfloat16


def split3(value):
    high = value.astype(bf16).astype(f32)
    rest = value - high
    middle = rest.astype(bf16).astype(f32)
    return high, middle, (rest - middle).astype(bf16).astype(f32)


def place(stat_lanes, column, request, base):
    lane = lax.broadcasted_iota(jnp.int32, stat_lanes.shape, 1)
    for part, piece in enumerate(split3(column)):
        stat_lanes = jnp.where(lane == base + part * STAT + request, piece, stat_lanes)
    return stat_lanes


def join3(tile):
    return tile + pltpu.roll(tile, LANES - STAT, 1) + pltpu.roll(tile, LANES - 2 * STAT, 1)


def attend_kernel(scalars_ref, q0, q1, q2, q3, own_ref, sib_ref, o0, o1, o2, o3, stat_ref, *, first, count):
    step = pl.program_id(0)
    length = scalars_ref[2 + first + step]
    outs = (o0, o1, o2, o3)
    query = jnp.concatenate([ref[...].reshape(-1, ref.shape[-1]) for ref in (q0, q1, q2, q3)], axis=0)
    rows = query.shape[0]
    block_len = own_ref.shape[2]
    scores = []
    for which, keys in enumerate((own_ref, sib_ref)):
        score = score_scale * jnp.dot(query, keys[0], preferred_element_type=f32)
        position = scalars_ref[which] * block_len + lax.broadcasted_iota(jnp.int32, (1, block_len), 1)
        scores.append(jnp.where(position < length, score, neg_floor))
    top = jnp.maximum(
        jnp.max(scores[0], axis=-1, keepdims=True), jnp.max(scores[1], axis=-1, keepdims=True)
    )
    shift = jnp.where(top <= neg_floor, 0.0, top)
    total = jnp.zeros((rows, 1), f32)
    result = jnp.zeros((rows, LATENT_WIDTH), f32)
    for score, keys in zip(scores, (own_ref, sib_ref)):
        probability = jnp.exp(score - shift)
        total = total + jnp.sum(probability, axis=-1, keepdims=True)
        result = result + lax.dot_general(
            probability.astype(bf16),
            keys[0, :LATENT_WIDTH],
            (((1,), (1,)), ((), ())),
            preferred_element_type=f32,
        )

    @pl.when(step == 0)
    def _():
        stat_ref[...] = jnp.zeros_like(stat_ref)

    stats = place(place(stat_ref[...], top, step, 0), total, step, 3 * STAT)
    stat_ref[...] = stats
    part = rows // 4
    pieces = part // 16
    for d, out in enumerate(outs):
        for chunk in range(LATENT_WIDTH // LANES):
            tile = result[d * part : (d + 1) * part, chunk * LANES : (chunk + 1) * LANES]
            out[:, step * 4 + chunk] = tile.astype(bf16).reshape(pieces, 16, LANES)

    @pl.when(step == count - 1)
    def _():
        for d, out in enumerate(outs):
            out[:, 4 * count] = stats[d * part : (d + 1) * part].astype(bf16).reshape(pieces, 16, LANES)


def attend(scalars, queries, cache, sibling, first, count):
    features, block_len = cache.shape[1:]
    tiles = 4 * count + 1
    out = jax.ShapeDtypeStruct((4, tiles, 16, LANES), bf16)
    rows = 4 * queries[0].shape[0] * 16
    return pl.pallas_call(
        functools.partial(attend_kernel, first=first, count=count),
        out_shape=[out] * 4,
        grid_spec=pltpu.PrefetchScalarGridSpec(
            num_scalar_prefetch=1,
            grid=(count,),
            in_specs=[pl.BlockSpec((4, None, 16, features), lambda i, *_: (0, i, 0, 0))] * 4
            + [pl.BlockSpec((1, features, block_len), lambda i, *_: (first + i, 0, 0))] * 2,
            out_specs=[pl.BlockSpec((4, tiles, 16, LANES), lambda i, *_: (0, 0, 0, 0))] * 4,
            scratch_shapes=[pltpu.VMEM((rows, LANES), f32)],
        ),
        compiler_params=pltpu.CompilerParams(
            dimension_semantics=("arbitrary",), vmem_limit_bytes=48 << 20
        ),
        name="attend",
    )(scalars, *queries, cache, sibling)


def merged_stats(tiles):
    joined = [join3(tile) for tile in tiles]
    sums = [pltpu.roll(one, LANES - 3 * STAT, 1) for one in joined]
    top = functools.reduce(jnp.maximum, joined)
    weights = [jnp.exp(one - top) for one in joined]
    total = sum(weight * one for weight, one in zip(weights, sums))
    return weights, top, total


def merge_kernel(a0, a1, a2, a3, o0, o1, o2, o3, *, count):
    refs = (a0, a1, a2, a3)
    for piece, out in enumerate((o0, o1, o2, o3)):
        weights, top, total = merged_stats([ref[piece, 4 * count].astype(f32) for ref in refs])
        stats = jnp.zeros((16, LANES), f32)
        for request in range(count):
            stats = place(stats, top[:, request : request + 1], request, 0)
            stats = place(stats, total[:, request : request + 1], request, 3 * STAT)
            shares = [weight[:, request : request + 1] for weight in weights]
            for chunk in range(4):
                tile = sum(
                    share * ref[piece, 4 * request + chunk].astype(f32)
                    for share, ref in zip(shares, refs)
                )
                out[4 * request + chunk] = tile.astype(bf16)
        out[4 * count] = stats.astype(bf16)


def merge(pieces, count):
    return pl.pallas_call(
        functools.partial(merge_kernel, count=count),
        out_shape=[jax.ShapeDtypeStruct((4 * count + 1, 16, LANES), bf16)] * 4,
        compiler_params=pltpu.CompilerParams(vmem_limit_bytes=32 << 20),
        name="merge",
    )(*pieces)


def project_kernel(core_ref, *refs, count):
    first, second = refs[0:4], refs[4:8]
    q_ref, keys_ref, up_ref, w_ref, kept_ref, given_ref, rows_ref = refs[8:]
    chunk = kept_ref.shape[2]

    tops, totals, results = [], [], []
    for half in (first, second):
        weights, top, total = merged_stats([ref[4 * count].astype(f32) for ref in half])
        for request in range(count):
            tops.append(top[:, request : request + 1])
            totals.append(total[:, request : request + 1])
            shares = [weight[:, request : request + 1] for weight in weights]
            results.append(
                jnp.concatenate(
                    [
                        sum(
                            share * ref[4 * request + part].astype(f32)
                            for share, ref in zip(shares, half)
                        )
                        for part in range(4)
                    ],
                    axis=1,
                )
            )
    cache_max = jnp.concatenate(tops, axis=0)
    cache_sum = jnp.concatenate(totals, axis=0)
    cache_result = jnp.concatenate(results, axis=0)
    rows = cache_max.shape[0]
    keys = keys_ref[...]
    near = score_scale * lax.dot_general(
        q_ref[...].reshape(rows, keys.shape[1]), keys, (((1,), (1,)), ((), ())), preferred_element_type=f32
    )
    row = lax.broadcasted_iota(jnp.int32, near.shape, 0)
    column = lax.broadcasted_iota(jnp.int32, near.shape, 1)
    seen = (row // 16 == column // 4) & (column % 4 <= (row % 16) // 4)
    near = jnp.where(seen, near, neg_floor)
    joint = jnp.maximum(cache_max, jnp.max(near, axis=-1, keepdims=True))
    rescale = jnp.exp(cache_max - joint)
    probability = jnp.where(seen, jnp.exp(near - joint), 0.0)
    denominator = cache_sum * rescale + jnp.sum(probability, axis=-1, keepdims=True)
    near_result = sum(
        jnp.dot(part.astype(bf16), keys[:, :LATENT_WIDTH], preferred_element_type=f32)
        for part in split3(probability)
    )
    latent = ((cache_result * rescale + near_result) / denominator).astype(bf16)
    grouped = rows // 4
    pick_row = lax.broadcasted_iota(jnp.int32, (grouped, rows), 0)
    pick_column = lax.broadcasted_iota(jnp.int32, (grouped, rows), 1)
    halves = grouped // 2
    core = core_ref[0]
    order = 2 * (pick_row % halves) + jnp.where(pick_row < halves, core, 1 - core)
    values = []
    for head in range(4):
        head_value = jnp.dot(latent, up_ref[head], preferred_element_type=f32).astype(bf16)
        pick = (pick_column == 4 * order + head).astype(f32).astype(bf16)
        values.append(jnp.dot(pick, head_value, preferred_element_type=f32).astype(bf16))
    values = jnp.concatenate(values, axis=1)
    for k in range(SPAN):
        block = jnp.dot(values, w_ref[:, k * chunk : (k + 1) * chunk], preferred_element_type=f32)
        for piece in range(chunk // LANES):
            rows_ref[piece, pl.ds(k, grouped, stride=SPAN), :] = block[:, piece * LANES : (piece + 1) * LANES]
    for piece in range(chunk // LANES):
        window = slice(piece * LANES, (piece + 1) * LANES)
        whole = rows_ref[piece].reshape(grouped, SPAN, LANES).astype(bf16)
        kept_ref[:, :, window] = whole[:halves]
        given_ref[:, :, window] = whole[halves:]


SPAN = 8


def project(core, first, second, own_query, new_keys, value_up, w_out, count):
    grouped = new_keys.shape[0]
    width = w_out.shape[1]
    out = jax.ShapeDtypeStruct((grouped // 2, SPAN, width // SPAN), bf16)
    inside = pl.BlockSpec(memory_space=pltpu.VMEM)
    return pl.pallas_call(
        functools.partial(project_kernel, count=count),
        out_shape=[out, out],
        in_specs=[pl.BlockSpec(memory_space=pltpu.SMEM)] + [inside] * 12,
        out_specs=[inside] * 2,
        scratch_shapes=[
            pltpu.VMEM((width // SPAN // LANES, grouped * SPAN, LANES), f32),
        ],
        compiler_params=pltpu.CompilerParams(vmem_limit_bytes=32 << 20),
        name="project",
    )(core, *first, *second, own_query, new_keys, value_up, w_out)


def spread_kernel(arrived_ref, residual_ref, gain_ref, attn_ref, stream_ref, normed_ref, rows_ref):
    attention = jnp.sum(arrived_ref[...].astype(f32), axis=0)
    attn_ref[...] = attention.astype(bf16)
    stream = (residual_ref[...].astype(f32) + attention).astype(bf16)
    stream_ref[...] = stream
    wide = stream.astype(f32)
    square = jnp.sum(jnp.sum(wide * wide, axis=1, keepdims=True), axis=0, keepdims=True)
    mean_square = square / (wide.shape[0] * wide.shape[1])
    normed = (wide * lax.rsqrt(mean_square + norm_eps) * gain_ref[...]).astype(bf16)
    normed_ref[...] = normed
    rows_ref[...] = jnp.broadcast_to(normed[None], rows_ref.shape)


def spread(arrived, residual, gain, chips):
    one = jax.ShapeDtypeStruct(residual.shape, bf16)
    rows = jax.ShapeDtypeStruct((chips,) + residual.shape, bf16)
    return pl.pallas_call(
        spread_kernel,
        out_shape=[one, one, one, rows],
        compiler_params=pltpu.CompilerParams(vmem_limit_bytes=32 << 20),
        name="spread",
    )(arrived, residual, gain)


def route_kernel(routes_ref, normed_ref, router_ref, coefficient_ref):
    products = router_ref[...].astype(f32) * normed_ref[...].astype(f32)[None]
    values = jnp.sum(jnp.sum(products, axis=2, keepdims=True), axis=1, keepdims=True)
    values = 1.0 / (1.0 + jnp.exp(-values))
    index = lax.broadcasted_iota(jnp.int32, values.shape, 0)
    chosen = jnp.zeros(values.shape, f32)
    for k in range(routes_ref.shape[1]):
        chosen = jnp.where(index == routes_ref[0, k], 1.0, chosen)
    picked = values * chosen
    share = route_scale * picked / jnp.sum(picked, axis=0, keepdims=True)
    coefficient_ref[...] = jnp.broadcast_to(share, coefficient_ref.shape)


def route(routes, normed, w_router):
    span, chunk = normed.shape
    inside = pl.BlockSpec(memory_space=pltpu.VMEM)
    return pl.pallas_call(
        route_kernel,
        out_shape=jax.ShapeDtypeStruct((EXPERTS, span, LANES), f32),
        in_specs=[pl.BlockSpec(memory_space=pltpu.SMEM), inside, inside],
        compiler_params=pltpu.CompilerParams(vmem_limit_bytes=16 << 20),
        name="route",
    )(routes, normed, w_router.T.reshape(EXPERTS, span, chunk))


def hold_kernel(*refs):
    count = len(refs) // 2
    sems = refs[-1]
    copies = []
    for i, (source, target) in enumerate(zip(refs[:count], refs[count : 2 * count])):
        part = source.shape[0] // SPAN
        for k in range(SPAN):
            window = pl.ds(k * part, part)
            copies.append(pltpu.make_async_copy(source.at[window], target.at[window], sems.at[i, k]))
    for copy in copies:
        copy.start()
    for copy in copies:
        copy.wait()


def hold(*weights):
    return pl.pallas_call(
        hold_kernel,
        out_shape=[pltpu.VMEM(w.shape, w.dtype) for w in weights],
        in_specs=[pl.BlockSpec(memory_space=pltpu.HBM)] * len(weights),
        out_specs=[pl.BlockSpec(memory_space=pltpu.VMEM)] * len(weights),
        scratch_shapes=[pltpu.SemaphoreType.DMA((len(weights), SPAN))],
        compiler_params=pltpu.CompilerParams(vmem_limit_bytes=24 << 20),
        name="hold",
    )(*[pltpu.with_memory_space_constraint(w, pltpu.HBM) for w in weights])


def experts_kernel(own_ref, sib_ref, gate_ref, up_ref, down_hbm, out_own, out_sib, down_ref, rows_ref, sems):
    half = own_ref.shape[0]
    rows = 2 * half
    chunk = out_own.shape[2]
    tiles = chunk // LANES

    def fetch(k):
        window = pl.ds(k * chunk, chunk)
        return pltpu.make_async_copy(down_hbm.at[:, window], down_ref.at[:, window], sems.at[k])

    for k in range(SPAN):
        fetch(k).start()
    for piece in range(tiles):
        window = slice(piece * LANES, (piece + 1) * LANES)
        rows_ref[piece, : half * SPAN] = own_ref[:, :, window].astype(f32).reshape(half * SPAN, LANES)
        rows_ref[piece, half * SPAN :] = sib_ref[:, :, window].astype(f32).reshape(half * SPAN, LANES)
    gate = up = 0.0
    for k in range(SPAN):
        block = jnp.concatenate(
            [rows_ref[piece, pl.ds(k, rows, stride=SPAN), :] for piece in range(tiles)], axis=1
        ).astype(bf16)
        gate = gate + jnp.dot(block, gate_ref[k * chunk : (k + 1) * chunk], preferred_element_type=f32)
        up = up + jnp.dot(block, up_ref[k * chunk : (k + 1) * chunk], preferred_element_type=f32)
    hidden = (gate / (1.0 + jnp.exp(-gate)) * up).astype(bf16)
    for k in range(SPAN):
        fetch(k).wait()
        result = jnp.dot(hidden, down_ref[:, k * chunk : (k + 1) * chunk], preferred_element_type=f32)
        for piece in range(tiles):
            rows_ref[piece, pl.ds(k, rows, stride=SPAN), :] = result[:, piece * LANES : (piece + 1) * LANES]
    for piece in range(tiles):
        window = slice(piece * LANES, (piece + 1) * LANES)
        out_own[:, :, window] = rows_ref[piece, : half * SPAN].reshape(half, SPAN, LANES).astype(bf16)
        out_sib[:, :, window] = rows_ref[piece, half * SPAN :].reshape(half, SPAN, LANES).astype(bf16)


def experts(own_rows, sibling_rows, w_gate, w_up, w_down):
    out = jax.ShapeDtypeStruct(own_rows.shape, bf16)
    inside = pl.BlockSpec(memory_space=pltpu.VMEM)
    half, span, chunk = own_rows.shape
    return pl.pallas_call(
        experts_kernel,
        out_shape=[out, out],
        in_specs=[inside] * 4 + [pl.BlockSpec(memory_space=pltpu.HBM)],
        out_specs=[inside] * 2,
        scratch_shapes=[
            pltpu.VMEM(w_down.shape, bf16),
            pltpu.VMEM((chunk // LANES, 2 * half * span, LANES), f32),
            pltpu.SemaphoreType.DMA((span,)),
        ],
        compiler_params=pltpu.CompilerParams(vmem_limit_bytes=20 << 20),
        name="experts",
    )(own_rows, sibling_rows, w_gate, w_up, pltpu.with_memory_space_constraint(w_down, pltpu.HBM))


def gather_kernel(returned_ref, stream_ref, coefficient_ref, out_ref):
    slices = returned_ref.shape[0] // EXPERTS
    for piece in range(stream_ref.shape[1] // LANES):
        window = slice(piece * LANES, (piece + 1) * LANES)
        total = jnp.zeros((SPAN, LANES), f32)
        for expert in range(EXPERTS):
            part = returned_ref[expert * slices : (expert + 1) * slices, :, window].astype(f32)
            total = total + coefficient_ref[expert] * jnp.sum(part, axis=0)
        out_ref[:, window] = (stream_ref[:, window].astype(f32) + total).astype(bf16)


def gather(returned, stream, coefficient):
    return pl.pallas_call(
        gather_kernel,
        out_shape=jax.ShapeDtypeStruct(stream.shape, bf16),
        compiler_params=pltpu.CompilerParams(vmem_limit_bytes=32 << 20),
        name="gather",
    )(returned, stream, coefficient)


def shift_by(value, axis, offset):
    size = lax.axis_size(axis)
    return lax.ppermute(value, axis, [(i, (i + offset) % size) for i in range(size)])


def all_shifts(value, axis):
    return [value] + [shift_by(value, axis, d) for d in range(1, lax.axis_size(axis))]


def return_shifts(pieces, axis):
    return [pieces[0]] + [shift_by(piece, axis, -d) for d, piece in enumerate(pieces) if d > 0]


def local(
    query,
    cache,
    new_keys,
    lengths,
    value_up_weight,
    w_out,
    residual,
    norm_gain,
    w_router,
    routes,
    w_gate,
    w_up,
    w_down,
):
    x, z, core = (lax.axis_index(name) for name in ("x", "z", "c"))
    ctx = (x * lax.axis_size("z") + z) * 2 + core
    requests = lengths.shape[0]
    features = query.shape[-1]
    width = w_out.shape[1]
    count = requests // 2
    cache = cache.swapaxes(1, 2)
    sibling_cache = shift_by(cache, "c", 1)
    own_query = query.reshape(requests, -1, features)
    stack_x = jnp.stack(all_shifts(own_query[:count], "x"))
    stack_z = jnp.stack(all_shifts(own_query[count:], "z"))
    stack_x, stack_z = lax.optimization_barrier((stack_x, stack_z))
    queries_a = all_shifts(stack_x, "z")
    queries_b = all_shifts(stack_z, "x")
    scalars = jnp.concatenate([jnp.stack([ctx, ctx ^ 1]).astype(jnp.int32), lengths])
    out_a = attend(scalars, queries_a, cache, sibling_cache, 0, count)
    out_b = attend(scalars, queries_b, cache, sibling_cache, count, count)
    half_a = merge(return_shifts(out_a, "z"), count)
    half_a = list(half_a)
    half_a[0], held_out = lax.optimization_barrier((half_a[0], w_out))
    (held_out,) = hold(held_out)
    final_a = return_shifts(half_a, "x")
    final_b = return_shifts(merge(return_shifts(out_b, "x"), count), "z")
    kept, given = project(
        core.astype(jnp.int32).reshape(1), final_a, final_b, own_query, new_keys, value_up_weight, held_out, count
    )
    chip_sum = (kept.astype(f32) + shift_by(given, "c", 1).astype(f32)).astype(bf16)
    arrived = lax.all_to_all(chip_sum, ("x", "z"), split_axis=0, concat_axis=0, tiled=True)
    chips = lax.axis_size("y") * lax.axis_size("x") * lax.axis_size("z")
    attn_out, stream, normed, rows = spread(
        arrived, residual.reshape(SPAN, -1), norm_gain.reshape(SPAN, -1), chips
    )
    normed, *weights = lax.optimization_barrier((normed, w_gate, w_up))
    weights = hold(*weights)
    coefficient = route(routes, normed, w_router)
    own_rows = lax.all_to_all(rows, ("y", "x", "z"), split_axis=0, concat_axis=0, tiled=True)
    own_rows, coefficient = lax.optimization_barrier((own_rows, coefficient))
    sibling_rows = shift_by(own_rows, "c", 1)
    out_own, out_sibling = experts(own_rows, sibling_rows, *weights, w_down)
    chip_out = (out_own.astype(f32) + shift_by(out_sibling, "c", 1).astype(f32)).astype(bf16)
    returned = lax.all_to_all(chip_out, ("y", "x", "z"), split_axis=0, concat_axis=0, tiled=True)
    layer_out = gather(returned, stream, coefficient)
    return (attn_out.reshape(1, width), layer_out.reshape(1, width))


def solution(mesh):
    names = ("y", "x", "z", "c")
    fine = Mesh(mesh.devices.reshape(4, 4, 4, 2), names)
    group, ctx = "y", ("x", "z", "c")
    return jax.shard_map(
        local,
        mesh=fine,
        in_specs=(
            P(group, ctx, None),
            P(group, ctx, None),
            P(group, None),
            P(group),
            P(ctx, None, None),
            P(ctx, None),
            P(names, None),
            P(),
            P(),
            P(names, None),
            P(None, names),
            P(None, names),
            P(names, None),
        ),
        out_specs=(P(names, None), P(names, None)),
        check_vma=False,
    )
```
